32 devices in a mesh: dp: 8 (over z, core), tp: 4 (over y, x).
Axes of the slice: x: 2, y: 2, z: 4, core: 2. Of those that a mesh axis runs over, the one named last changes fastest.
Arguments:
- student_hidden: bfloat16 [1152, 3456], P('dp'), may hold values from -6 to 6
- norm_gain: float32 [3456], replicated, may hold values from 0.25 to 1.75
- projection: bfloat16 [3456, 8192], P(None, 'tp'), may hold values from -0.109375 to 0.109375
- teacher_partials: bfloat16 [4, 1152, 8192], P('tp', 'dp'), may hold values from -5 to 5
- teacher_residual: bfloat16 [1152, 8192], P('dp', 'tp'), may hold values from -90 to 90
- owner: int32 [1152], P('dp'), may hold values from 0 to 1151, as said below
Outputs:
- grad_scaled: float32 [3456, 8192], P('dp', 'tp')
The draws below stay inside these ranges and needn't reach their ends.
Inputs may be any that keep to these rules, and one draw needn't show every extreme that they name: owner is a permutation of all token indices; the 144 teacher rows of each index of dp hold exactly 18 tokens owned by each index of dp.
All inputs are finite; a program needn't handle non-finite values.
Results may differ from the reference program's by a relative error of at most 0.009.
Values may be sent and summed in bfloat16 or wider, within the bound.
A program may use at most 128 MiB of HBM per device.

```python
import jax
import jax.numpy as jnp
from jax import lax

DS = 3456
DTW = 8192
TOK_DEV = 144
TOKENS = 1152
N_DP = 8
N_TP = 4


def draw_owner(key, part):
    blocks = TOKENS // TOK_DEV
    slots = TOK_DEV // blocks
    keys = jax.random.split(jax.random.fold_in(key, 17), 2 * blocks)
    source_perms = jax.vmap(lambda k: jax.random.permutation(k, TOK_DEV))(keys[:blocks])
    target_perms = jax.vmap(lambda k: jax.random.permutation(k, TOK_DEV))(keys[blocks:])
    dest = source_perms // slots
    within = source_perms % slots
    column = jnp.arange(blocks, dtype=jnp.int32)[:, None] * slots + within
    local = target_perms[dest, column]
    return (dest * TOK_DEV + local).reshape(-1).astype(jnp.int32)


def draw_teacher_residual(key, part):
    first, second, third = jax.random.split(jax.random.fold_in(key, 29), 3)
    row_pos = jnp.arange(TOKENS, dtype=jnp.float32) / TOKENS
    col_pos = jnp.arange(DTW, dtype=jnp.float32) / DTW
    row_jitter = jnp.exp(jax.random.uniform(second, (TOKENS,), jnp.float32, -0.3, 0.3))
    col_jitter = jnp.exp(jax.random.uniform(third, (DTW,), jnp.float32, -0.3, 0.3))
    base = jnp.clip(jax.random.normal(first, (TOKENS, DTW), jnp.float32), -4.0, 4.0)
    row_scale = 0.2 * 20.0 ** row_pos * row_jitter
    col_scale = 3.0 ** col_pos * col_jitter
    return (base * row_scale[:, None] * col_scale[None, :]).astype(jnp.bfloat16)


def spiked(array, key, source, target, parts, factor):
    def block_of(dim):
        return (jnp.arange(array.shape[dim]) // (array.shape[dim] // parts)).reshape((-1,) + (1,) * (array.ndim - 1 - dim))

    one_side = jax.random.permutation(key, parts)[block_of(target)]
    other_side = (block_of(target) + parts // 2) % parts
    return jnp.where((block_of(source) == one_side) | (block_of(source) == other_side), factor * array, array)


def steps_of(stream_key, dims, pieces, low, largest):
    def one(axis_at, parts):
        draws = jax.random.uniform(jax.random.fold_in(jax.random.fold_in(stream_key, 6), axis_at), (parts,), jnp.float32, low / len(pieces), largest / len(pieces))
        return jnp.repeat(jnp.exp(draws), dims[axis_at] // parts).reshape((-1,) + (1,) * (len(dims) - axis_at - 1))

    factor_of = one(*pieces[0])
    for cut in pieces[1:]:
        factor_of = factor_of * one(*cut)
    return factor_of


def gaussian(key, shape, scale, most, cuts=(), kind=jnp.bfloat16):
    factor_of = steps_of(key, shape, cuts, -0.22, 0.18) if cuts else 1.0
    array = jax.random.normal(key, shape, jnp.float32) * scale * factor_of
    return jnp.minimum(jnp.maximum(array, -most), most).astype(kind)


def noise_with(stream_key, shape, width, most, shards, heavy, held_as=jnp.bfloat16):
    values = width * jax.random.normal(stream_key, shape, jnp.float32)
    if shards:
        values = values * steps_of(stream_key, shape, shards, -0.22, 0.18)
    return jnp.clip(spiked(values, jax.random.fold_in(stream_key, 3), *heavy), -most, most).astype(held_as)


def setup_inputs(seed: int = 0) -> dict:
    arg_keys = jax.random.split(jax.random.key(seed), 7)
    return {
        "student_hidden": gaussian(arg_keys[0], (TOKENS, DS), 1.0, 6.0, ((0, 8),)),
        "norm_gain": jnp.clip(1.0 + 0.15 * jax.random.normal(arg_keys[1], (DS,), jnp.float32), 0.25, 1.75),
        "projection": gaussian(arg_keys[2], (DS, DTW), DS ** -0.5, 0.109375, ((1, 4),)),
        "teacher_partials": noise_with(arg_keys[3], (N_TP, TOKENS, DTW), 0.25, 5.0, ((0, 4), (1, 8)), (0, 2, 4, 2.0)),
        "teacher_residual": draw_teacher_residual(jax.random.fold_in(arg_keys[6], 71), 0),
        "owner": draw_owner(jax.random.fold_in(arg_keys[6], 71), 0),
    }


def block_partial(pair):
    normed_block, diff_block = pair
    return lax.dot_general(normed_block, diff_block, (((0,), (0,)), ((), ())), preferred_element_type=jnp.float32)

def reference(student_hidden, norm_gain, projection, teacher_partials, teacher_residual, owner):

    def add_rank(index, total):
        return total + lax.dynamic_index_in_dim(teacher_partials, index, 0, keepdims=False).astype(jnp.float32)
    summed = lax.fori_loop(0, N_TP, add_rank, jnp.zeros((TOKENS, DTW), jnp.float32))
    teacher = (teacher_residual.astype(jnp.float32) + summed).astype(jnp.bfloat16)
    target = jnp.zeros((TOKENS, DTW), jnp.bfloat16).at[owner.astype(jnp.int32)].set(teacher)
    values = student_hidden.astype(jnp.float32)
    inverse = lax.rsqrt(lax.optimization_barrier(jnp.mean(values * values, axis=-1, keepdims=True)) + 1e-05)
    normed = (values * inverse * norm_gain).astype(jnp.bfloat16)
    pred = jnp.dot(normed, projection, preferred_element_type=jnp.float32)
    diff = (pred - target.astype(jnp.float32)).astype(jnp.bfloat16)
    normed_blocks = normed.reshape(N_DP, TOK_DEV, DS)
    diff_blocks = diff.reshape(N_DP, TOK_DEV, DTW)
    maxima = lax.map(lambda pair: jnp.max(jnp.abs(block_partial(pair))), (normed_blocks, diff_blocks))
    scale = jnp.max(maxima) + 1e-06

    def accumulate(total, pair):
        rounded = lax.optimization_barrier((block_partial(pair) / scale).astype(jnp.bfloat16))
        return (total + rounded.astype(jnp.float32), None)
    grad_scaled, unused = lax.scan(accumulate, jnp.zeros((DS, DTW), jnp.float32), (normed_blocks, diff_blocks))
    return grad_scaled
```

```python
import functools

import jax
import jax.numpy as jnp
from jax import lax
from jax.experimental import pallas as pl
from jax.experimental.pallas import tpu as pltpu
from jax.sharding import PartitionSpec as P

MESH = pl.DeviceIdType.MESH


def greet(groups):
    barrier = pltpu.get_barrier_semaphore()
    total = 0
    for axis, size in groups:
        me = lax.axis_index(axis)
        for step in range(1, size):
            pl.semaphore_signal(
                barrier, inc=1, device_id={axis: lax.rem(me + step, size)}, device_id_type=MESH
            )
        total += size - 1
    pl.semaphore_wait(barrier, total)


def remote(src, dst, send_sem, recv_sem, axis, target):
    return pltpu.make_async_remote_copy(
        src_ref=src,
        dst_ref=dst,
        send_sem=send_sem,
        recv_sem=recv_sem,
        device_id={axis: target},
        device_id_type=MESH,
    )


def exchange(axis, size, pick, dst, send_sem, recv_sem):
    me = lax.axis_index(axis)
    copies = []
    for step in range(1, size):
        peer = lax.rem(me + step, size)
        copies.append(
            remote(
                pick(peer), dst.at[me], send_sem.at[step], recv_sem.at[step], axis, peer
            )
        )
    return copies


def first_kernel(
    n, t, terms, blocks, index, terms_out, blocks_out, index_out,
    hold_terms, hold_blocks, hold_index, local_sem, t_send, t_recv, b_send, b_recv, i_send, i_recv,
):
    width = terms_out.shape[2]
    me_t, me_d = lax.axis_index("tp"), lax.axis_index("dp")

    def columns(peer):
        return terms.at[:, pl.ds(pl.multiple_of(peer * width, 128), width)]

    loads = [
        pltpu.make_async_copy(columns(me_t), hold_terms, local_sem.at[0]),
        pltpu.make_async_copy(blocks.at[me_d], hold_blocks, local_sem.at[1]),
        pltpu.make_async_copy(index.at[me_d], hold_index, local_sem.at[2]),
    ]
    for load in loads:
        load.start()
    greet((("tp", t), ("dp", n)))
    copies = exchange("tp", t, columns, terms_out, t_send, t_recv)
    copies += exchange("dp", n, lambda peer: index.at[peer], index_out, i_send, i_recv)
    copies += exchange("dp", n, lambda peer: blocks.at[peer], blocks_out, b_send, b_recv)
    for copy in copies:
        copy.start()
    stores = [
        pltpu.make_async_copy(hold_terms, terms_out.at[me_t], local_sem.at[3]),
        pltpu.make_async_copy(hold_blocks, blocks_out.at[me_d], local_sem.at[4]),
        pltpu.make_async_copy(hold_index, index_out.at[me_d], local_sem.at[5]),
    ]
    for load, store in zip(loads, stores):
        load.wait()
        store.start()
    for store in stores:
        store.wait()
    for copy in copies:
        copy.wait()


def rows_kernel(n, rows, rows_out, hold, local_sem, send, recv):
    me = lax.axis_index("dp")
    load = pltpu.make_async_copy(rows.at[me], hold, local_sem.at[0])
    load.start()
    greet((("dp", n),))
    copies = exchange("dp", n, lambda peer: rows.at[peer], rows_out, send, recv)
    for copy in copies:
        copy.start()
    load.wait()
    store = pltpu.make_async_copy(hold, rows_out.at[me], local_sem.at[1])
    store.start()
    store.wait()
    for copy in copies:
        copy.wait()


def last_kernel(
    n, t, pieces, diff, blocks, out,
    errors, partials, largest, mine_t, mine_d, from_t, from_d,
    local_sem, send, recv, mt_send, mt_recv, md_send, md_recv,
):
    me = lax.axis_index("dp")
    chip, core = me // 2, me % 2
    chips = n // 2
    other = 1 - core
    partner = chip * 2 + other
    width = errors.shape[3]
    features = out.shape[0]

    def piece(source, q, way, target):
        return remote(
            errors.at[source, q], errors.at[source, q],
            send.at[source, q, way], recv.at[source, q], "dp", target,
        )

    def local(q):
        return pltpu.make_async_copy(
            diff.at[:, pl.ds(pl.multiple_of(q * width, 128), width)],
            errors.at[me, q], local_sem.at[q],
        )

    for q in range(pieces):
        local(q).start()
    largest[...] = jnp.zeros_like(largest)
    greet((("tp", t), ("dp", n)))
    for q in range(pieces):
        local(q).wait()

        @pl.when(chip > 0)
        def _():
            piece(me, q, 0, me - 2).start()

        @pl.when(chip < chips - 1)
        def _():
            piece(me, q, 1, me + 2).start()

        piece(me, q, 2, partner).start()

    def compute(source, q):
        value = jnp.dot(blocks[source], errors[source, q], preferred_element_type=jnp.float32)
        partials[source, q] = value
        folded = jnp.max(jnp.abs(value).reshape(features // 8, 8, width), axis=0)
        largest[...] = jnp.maximum(largest[...], folded)

    @pl.loop(0, pieces)
    def _(q):
        compute(me, q)

    def arrive(i, _):
        step, q = i // pieces + 1, i % pieces
        left, right = me - 2 * step, me + 2 * step

        @pl.when(chip >= step)
        def _():
            piece(left, q, 1, partner).wait_recv()
            piece(left, q, 2, partner).start()

            @pl.when(chip < chips - 1)
            def _():
                piece(left, q, 1, me + 2).start()

        @pl.when(chip + step < chips)
        def _():
            piece(right, q, 0, partner).wait_recv()
            piece(right, q, 2, partner).start()

            @pl.when(chip > 0)
            def _():
                piece(right, q, 0, me - 2).start()

        @pl.when(chip >= step)
        def _():
            compute(left, q)

        @pl.when(chip + step < chips)
        def _():
            compute(right, q)

        return 0

    lax.fori_loop(0, (chips - 1) * pieces, arrive, 0)

    @pl.loop(0, chips * pieces)
    def _(i):
        source, q = (i // pieces) * 2 + other, i % pieces
        piece(source, q, 2, partner).wait_recv()
        compute(source, q)

    tile = mine_t.shape
    mine_t[...] = jnp.broadcast_to(jnp.max(largest[...]), tile)
    copies = exchange("tp", t, lambda peer: mine_t, from_t, mt_send, mt_recv)
    for copy in copies:
        copy.start()
    best = mine_t[...]
    for step in range(1, t):
        copies[step - 1].wait()
        best = jnp.maximum(best, from_t[lax.rem(lax.axis_index("tp") + t - step, t)])
    mine_d[...] = best
    copies = exchange("dp", n, lambda peer: mine_d, from_d, md_send, md_recv)
    for copy in copies:
        copy.start()
    for step in range(1, n):
        copies[step - 1].wait()
        best = jnp.maximum(best, from_d[lax.rem(me + n - step, n)])
    inverse = 1.0 / (jnp.max(best) + 1e-06)

    high = 16 if features % 16 == 0 else 8

    @pl.loop(0, features // high)
    def _(block):
        rows = pl.ds(pl.multiple_of(block * high, high), high)
        for q in range(pieces):
            total = jnp.zeros((high, width), jnp.float32)
            for source in range(n):
                term = (partials[source, q, rows, :] * inverse).astype(jnp.bfloat16)
                total = total + term.astype(jnp.float32)
            out[rows, pl.ds(q * width, width)] = total

    @pl.loop(0, chips * pieces)
    def _(i):
        source_chip, q = i // pieces, i % pieces
        source = source_chip * 2 + core
        piece(source, q, 2, partner).wait_send()

        @pl.when((source_chip >= chip) & (chip > 0))
        def _():
            piece(source, q, 0, me - 2).wait_send()

        @pl.when((source_chip <= chip) & (chip < chips - 1))
        def _():
            piece(source, q, 1, me + 2).wait_send()


def dma(*shape):
    return pltpu.SemaphoreType.DMA(shape)


def call(kernel, collective_id, operands, in_specs, out_shape, out_specs, scratch, flops=0):
    return pl.pallas_call(
        kernel,
        out_shape=out_shape,
        in_specs=in_specs,
        out_specs=out_specs,
        scratch_shapes=scratch,
        compiler_params=pltpu.CompilerParams(
            collective_id=collective_id, has_side_effects=True
        ),
    )(*operands)


def per_device(student_hidden, norm_gain, projection, teacher_partials, teacher_residual, owner):
    columns = projection.shape[1]
    rows_dev, features_all = student_hidden.shape
    n, t = lax.axis_size("dp"), lax.axis_size("tp")
    slots = rows_dev // n
    share = features_all // n
    wide = -(-share // 128) * 128
    hbm = pl.BlockSpec(memory_space=pl.ANY)
    vmem = pl.BlockSpec(memory_space=pltpu.VMEM)
    bf16, f32, i32 = jnp.bfloat16, jnp.float32, jnp.int32

    order = jnp.argsort(owner // rows_dev, stable=True)
    index = jnp.pad(owner[order].reshape(n, 1, slots), ((0, 0), (0, 0), (0, 128 - slots)))
    values = student_hidden.astype(f32)
    inverse = lax.rsqrt(jnp.mean(values * values, axis=-1, keepdims=True) + 1e-05)
    normed = (values * inverse * norm_gain).astype(bf16)
    blocks = jnp.pad(
        normed.reshape(rows_dev, n, share).transpose(1, 0, 2), ((0, 0), (0, 0), (0, wide - share))
    )
    terms, arrived_blocks, arrived_index = call(
        functools.partial(first_kernel, n, t), 0,
        (teacher_partials[0], blocks, index),
        [hbm] * 3,
        [
            jax.ShapeDtypeStruct((t, rows_dev, columns), bf16),
            jax.ShapeDtypeStruct((n, rows_dev, wide), bf16),
            jax.ShapeDtypeStruct((n, 1, 128), i32),
        ],
        [hbm] * 3,
        [
            pltpu.VMEM((rows_dev, columns), bf16),
            pltpu.VMEM((rows_dev, wide), bf16),
            pltpu.VMEM((1, 128), i32),
            dma(6), dma(t), dma(t), dma(n), dma(n), dma(n), dma(n),
        ],
    )
    summed = jnp.sum(terms.astype(f32), axis=0)
    teacher = (teacher_residual.astype(f32) + summed).astype(bf16)
    outgoing = teacher[order].reshape(n, slots, columns)
    arrived = call(
        functools.partial(rows_kernel, n), 1,
        (outgoing,),
        [hbm],
        jax.ShapeDtypeStruct((n, slots, columns), bf16),
        hbm,
        [pltpu.VMEM((slots, columns), bf16), dma(2), dma(n), dma(n)],
    )
    placing = jnp.argsort(arrived_index[:, 0, :slots].reshape(-1) % rows_dev)
    target = arrived.reshape(rows_dev, columns)[placing]
    pred = jnp.dot(normed, projection, preferred_element_type=f32)
    diff = (pred - target.astype(f32)).astype(bf16)
    turned = arrived_blocks[:, :, :share].transpose(0, 2, 1)
    pieces = 4 if columns % 512 == 0 and columns >= 2048 else 1
    width = columns // pieces
    return call(
        functools.partial(last_kernel, n, t, pieces), 2,
        (diff, turned),
        [hbm, vmem],
        jax.ShapeDtypeStruct((share, columns), f32),
        vmem,
        [
            pltpu.VMEM((n, pieces, rows_dev, width), bf16),
            pltpu.VMEM((n, pieces, share, width), f32),
            pltpu.VMEM((8, width), f32),
            pltpu.VMEM((8, 128), f32),
            pltpu.VMEM((8, 128), f32),
            pltpu.VMEM((t, 8, 128), f32),
            pltpu.VMEM((n, 8, 128), f32),
            dma(pieces), dma(n, pieces, 3), dma(n, pieces), dma(t), dma(t), dma(n), dma(n),
        ],
    )


def solution(mesh):
    placed = (P("dp", None), P(), P(None, "tp"), P("tp", "dp", None), P("dp", "tp"), P("dp"))
    return jax.shard_map(
        per_device, mesh=mesh, in_specs=placed, out_specs=P("dp", "tp"), check_vma=False
    )
```
